32 devices in a mesh: row: 8 (over y, x, core), col: 4 (over z).
Axes of the slice: x: 2, y: 2, z: 4, core: 2. Of those that a mesh axis runs over, the one named last changes fastest.
Arguments:
- three_centre: float32 [8, 1024, 18432], P('row', None, 'col'), may hold values from -6 to 6
- occupied: float32 [8, 1024, 128], P('row'), may hold values from -0.1875 to 0.1875
- virtual: float32 [8, 1024, 128], P('row'), may hold values from -0.005859375 to 0.005859375
- tile_map: int32 [8, 144], P('row', 'col'), may hold values from 0 to 1, as said below
Outputs:
- polarizability: float32 [18432, 18432], P('row', 'col')
The draws below stay inside these ranges and needn't reach their ends.
Inputs may be any that keep to these rules, and one draw needn't show every extreme that they name: `tile_map`: 0 or 1; the share of ones differs from orbital to orbital.
All inputs are finite; a program needn't handle non-finite values.
Results may differ from the reference program's by a relative error of at most 0.000071.
Values sent between devices are 32-bit elements; how exact they have to be, the bound alone decides.
No kernel may reach another device: no remote copies, remote signals or barrier semaphores. Data moves between devices by JAX's collectives and lax.ppermute only.
A program may use at most 192 MiB of HBM per device.

```python
import jax
import jax.numpy as jnp
from jax import lax

AUX = 18432
AB = 128
NB = 1024
NU = 128
MU = 8
PAIRS = 1024
NAB = 144


def draw_tile_map(key, part):
    filling_key, ticket_key = jax.random.split(jax.random.fold_in(key, 7))
    filling = jax.random.randint(filling_key, (MU, 1), 1, 5)
    ticket = jax.random.randint(ticket_key, (MU, NAB), 0, 5)
    return (ticket < filling).astype(jnp.int32)


def levels(own_key, extent, cuts, low, top_value):
    gain, own = 1.0, jax.random.fold_in(own_key, 6)
    for axis_at, parts in cuts:
        draws = jnp.exp(jax.random.uniform(jax.random.fold_in(own, axis_at), (parts,), jnp.float32, low / len(cuts), top_value / len(cuts)))
        gain = gain * jnp.repeat(draws, extent[axis_at] // parts).reshape([-1 if axis == axis_at else 1 for axis in range(len(extent))])
    return gain


def bell_draw(rng, extent, deviation, most, cuts=(), held_as=jnp.bfloat16):
    array = deviation * jax.random.normal(rng, extent, jnp.float32)
    if cuts:
        array = array * levels(rng, extent, cuts, -0.22, 0.18)
    return jnp.clip(array, -most, most).astype(held_as)


def setup_inputs(seed: int = 0) -> dict:
    arg_keys = jax.random.split(jax.random.key(seed), 5)
    return {
        "three_centre": bell_draw(arg_keys[0], (MU, NB, AUX), 1.0, 6.0, ((0, 8), (2, 4)), jnp.float32),
        "occupied": bell_draw(arg_keys[1], (MU, NB, NU), NB ** -0.5, 0.1875, ((0, 8),), jnp.float32),
        "virtual": bell_draw(arg_keys[2], (MU, NB, NU), (NB * PAIRS) ** -0.5, 0.005859375, ((0, 8),), jnp.float32),
        "tile_map": draw_tile_map(jax.random.fold_in(arg_keys[4], 71), 0),
    }


def contract_pairs(density, tensor):
    product = jnp.einsum("mnl,mnp->mlp", density, tensor, precision=lax.Precision.HIGHEST)
    return product.reshape(product.shape[0] * product.shape[1], product.shape[2])


def reference(three_centre, occupied, virtual, tile_map):
    keep_factor = jnp.repeat(tile_map.astype(jnp.float32), AB, axis=1)
    masked = three_centre * keep_factor[:, None, :]
    occupied_pairs = contract_pairs(occupied.astype(jnp.float32), masked)
    virtual_pairs = contract_pairs(virtual.astype(jnp.float32), masked)
    return lax.dot_general(occupied_pairs, virtual_pairs, (((0,), (0,)), ((), ())), precision=lax.Precision.HIGHEST, preferred_element_type=jnp.float32)
```

```python
import math

import jax
import jax.numpy as jnp
from jax import lax
from jax.experimental import pallas as pl
from jax.experimental.pallas import tpu as pltpu
from jax.sharding import PartitionSpec as P

F32 = jnp.float32
BF16 = jnp.bfloat16
SHARES = (2, 2, 2, 2, 1)
DIRECT = (1, 3, 4)
SMALL_VMEM = 14 * 1024 * 1024
LARGE_VMEM = 48 * 1024 * 1024
CORES = 2


def two_parts(value):
    top = value.astype(BF16)
    return top, (value - top.astype(F32)).astype(BF16)


def dot(left, right):
    return jnp.dot(left, right, preferred_element_type=F32)


def three_products(stacked, right):
    rows = stacked.shape[0] // 2
    top, rest = right
    if rows < 512:
        first = dot(stacked[...], top)
        return first[:rows] + (first[rows:] + dot(stacked[:rows], rest))
    return (dot(stacked[:rows], rest) + dot(stacked[rows:], top)) + dot(stacked[:rows], top)


def params(limit=SMALL_VMEM):
    return pltpu.CompilerParams(vmem_limit_bytes=limit)


def stage_one(core, tensor, occupied, virtual, keep, unit, width, first, chunks):
    _, basis, columns = tensor.shape
    partners = occupied.shape[2]
    halves = columns // width
    count = sum(chunks)
    starts = [sum(chunks[:i]) for i in range(len(chunks))]
    per_half = width // unit

    def half_of(i, core_ref):
        return (core_ref[0] + 1 + i // count) % halves

    def kernel(core_ref, t_ref, o_ref, v_ref, k_ref, *rest):
        outs, v_out, left = rest[: 2 * len(chunks)], rest[-2], rest[-1]
        step = pl.program_id(0)

        @pl.when(step == 0)
        def _():
            both = jnp.concatenate([o_ref[0].T, v_ref[0].T], axis=0)
            left[: 2 * partners], left[2 * partners :] = two_parts(both)

        product = three_products(left, two_parts(t_ref[0])) * k_ref[...]
        v_out[...] = product[partners:]
        turn, at = step // count, step % count
        for i, out in enumerate(outs):
            chunk = i // 2

            @pl.when((turn == i % 2) & (at >= starts[chunk]) & (at < starts[chunk] + chunks[chunk]))
            def _(out=out):
                out[...] = product[:partners]

    def column(i, core_ref):
        return half_of(i, core_ref) * per_half + first + i % count

    o_specs = [
        pl.BlockSpec((partners, unit), lambda i, _, s=s + t * count, c=c: (0, jnp.clip(i - s, 0, c - 1)))
        for s, c in zip(starts, chunks)
        for t in range(2)
    ]
    v_spec = pl.BlockSpec((partners, unit), lambda i, ref: (0, half_of(i, ref) * count + i % count))
    outs = pl.pallas_call(
        kernel,
        grid_spec=pltpu.PrefetchScalarGridSpec(
            num_scalar_prefetch=1,
            grid=(halves * count,),
            in_specs=[
                pl.BlockSpec((1, basis, unit), lambda i, ref: (0, 0, column(i, ref))),
                pl.BlockSpec((1, basis, partners), lambda i, ref: (0, 0, 0)),
                pl.BlockSpec((1, basis, partners), lambda i, ref: (0, 0, 0)),
                pl.BlockSpec((1, unit), lambda i, ref: (0, column(i, ref))),
            ],
            out_specs=o_specs + [v_spec],
            scratch_shapes=[pltpu.VMEM((4 * partners, basis), BF16)],
        ),
        out_shape=[jax.ShapeDtypeStruct((partners, c * unit), F32) for c in chunks for _ in range(2)]
        + [jax.ShapeDtypeStruct((partners, halves * count * unit), F32)],
        compiler_params=params(LARGE_VMEM),
        cost_estimate=pl.CostEstimate(
            flops=12 * partners * basis * halves * count * unit,
            bytes_accessed=4 * basis * halves * count * unit,
            transcendentals=0,
        ),
        name="stage_one",
    )(core, tensor, occupied, virtual, keep)
    return [(outs[2 * i], outs[2 * i + 1]) for i in range(len(chunks))], outs[-1]


def choose(place, sources, count):
    shape = sources[0].shape

    def kernel(place_ref, *refs):
        ins, outs, sems = refs[: len(sources)], refs[len(sources) : -1], refs[-1]
        for d, out in enumerate(outs):
            for e, ref in enumerate(ins):
                @pl.when((place_ref[0] ^ d ^ place_ref[1]) == e)
                def _(ref=ref, out=out, d=d):
                    pltpu.make_async_copy(ref, out, sems.at[d]).start()

        for d, out in enumerate(outs):
            pltpu.make_async_copy(ins[0], out, sems.at[d]).wait()

    return pl.pallas_call(
        kernel,
        in_specs=[pl.BlockSpec(memory_space=pltpu.SMEM)] + [pl.BlockSpec(memory_space=pl.ANY)] * len(sources),
        out_specs=[pl.BlockSpec(memory_space=pltpu.VMEM)] * count,
        out_shape=[jax.ShapeDtypeStruct(shape, F32)] * count,
        scratch_shapes=[pltpu.SemaphoreType.DMA((count,))],
        compiler_params=params(),
        name="choose",
    )(place, *sources)


def split_rows(pieces):
    partners, count = pieces[0].shape
    pairs = partners * len(pieces)
    block = math.gcd(count, 512)

    def kernel(*refs):
        ins, (top, rest) = refs[: len(pieces)], refs[-2:]
        at = pl.ds(pl.multiple_of(pl.program_id(0) * block, block), block)
        for i, ref in enumerate(ins):
            rows = pl.ds(i * partners, partners)
            top[rows, at], rest[rows, at] = two_parts(ref[...])

    return pl.pallas_call(
        kernel,
        grid=(count // block,),
        in_specs=[pl.BlockSpec((partners, block), lambda i: (0, i))] * len(pieces),
        out_specs=[pl.BlockSpec(memory_space=pltpu.VMEM)] * 2,
        out_shape=[pltpu.VMEM((pairs, count), BF16)] * 2,
        compiler_params=params(SMALL_VMEM),
        cost_estimate=pl.CostEstimate(flops=4 * pairs * count, bytes_accessed=8 * pairs * count, transcendentals=0),
        name="split_rows",
    )(*pieces)


def product_rows(pieces, groups, held, rows, width, unit, offset):
    each, partners, count = pieces[0].shape
    pairs = each * partners * len(pieces)
    columns = sum(top.shape[1] for _, top, _ in groups)
    halves = columns // width
    held = () if held is None else (held,)
    block = 2 * unit
    for _, top, _ in groups:
        block = math.gcd(block, top.shape[1])
    tiles = columns // block

    def kernel(*refs):
        ins = refs[: len(pieces)]
        sides = refs[len(pieces) : len(pieces) + 2 * len(groups)]
        out, landed, left, ready, in_sems, out_sems = refs[-6:]

        def fetch(i):
            return pltpu.make_async_copy(ins[i], landed.at[i], in_sems.at[i])

        def finish(slot):
            place = out.at[pl.ds(offset, count), pl.ds(0, block)]
            pltpu.make_async_copy(ready.at[slot], place, out_sems.at[slot]).wait()

        for i in range(len(pieces)):
            fetch(i).start()
        for i in range(len(pieces)):
            fetch(i).wait()
            for e in range(each):
                at = pl.ds((i * each + e) * partners, partners)
                left[:count, at], left[count:, at] = two_parts(landed[i, e].T)

        begin = 0
        for g, (first, top, _) in enumerate(groups):
            steps = top.shape[1] // block
            per_half = top.shape[1] // unit // halves

            def step(i, carry, g=g, first=first, begin=begin, per_half=per_half):
                slot = (begin + i) % 2

                @pl.when(begin + i >= 2)
                def _():
                    finish(slot)

                at = pl.ds(pl.multiple_of(i * block, block), block)
                ready[slot] = three_products(left, (sides[2 * g][:, at], sides[2 * g + 1][:, at]))
                for n in range(block // unit):
                    u = i * (block // unit) + n
                    column = pl.multiple_of(u // per_half * width + first + u % per_half * unit, unit)
                    place = out.at[pl.ds(offset, count), pl.ds(column, unit)]
                    part = ready.at[slot, :, pl.ds(n * unit, unit)]
                    pltpu.make_async_copy(part, place, out_sems.at[slot]).start()
                return carry

            lax.fori_loop(0, steps, step, 0)
            begin += steps
        for i in range(max(tiles - 2, 0), tiles):
            finish(i % 2)

    return pl.pallas_call(
        kernel,
        in_specs=[pl.BlockSpec(memory_space=pl.ANY)] * len(pieces)
        + [pl.BlockSpec(memory_space=pltpu.VMEM)] * (2 * len(groups))
        + [pl.BlockSpec(memory_space=pl.ANY)] * len(held),
        out_specs=pl.BlockSpec(memory_space=pl.ANY),
        out_shape=jax.ShapeDtypeStruct((rows, columns), F32),
        scratch_shapes=[
            pltpu.VMEM((len(pieces), each, partners, count), F32),
            pltpu.VMEM((2 * count, pairs), BF16),
            pltpu.VMEM((2, count, block), F32),
            pltpu.SemaphoreType.DMA((len(pieces),)),
            pltpu.SemaphoreType.DMA((2,)),
        ],
        input_output_aliases={len(pieces) + 2 * len(groups): 0} if held else {},
        compiler_params=params(SMALL_VMEM),
        cost_estimate=pl.CostEstimate(
            flops=6 * pairs * count * columns,
            bytes_accessed=4 * pairs * columns + 4 * count * columns,
            transcendentals=0,
        ),
        name="product_rows",
    )(*pieces, *[side for _, top, rest in groups for side in (top, rest)], *held)


def solution(mesh):
    n_row, n_col = mesh.shape["row"], mesh.shape["col"]
    chips = n_row // CORES
    square = chips == 4

    def swap(value, bits):
        return lax.ppermute(value, "row", [(r, r ^ bits) for r in range(n_row)])

    def along_columns(value, direct):
        got, bit = {0: value}, n_col // 2
        while bit:
            for e in list(got):
                source, hop = (value, e + bit) if direct else (got[e], bit)
                got[e + bit] = lax.ppermute(source, "col", [(c, c ^ hop) for c in range(n_col)])
            bit //= 2
        return [got[e] for e in range(n_col)]

    def gather_rows(value, core):
        got = {0: value}
        if square:
            got[2] = swap(value, 2)
            got[4] = swap(value, 4)
            relay = jnp.where(core == 0, got[2], got[4])
            got[6] = lax.ppermute(relay, "row", [(r, r ^ (2 if r % CORES else 4)) for r in range(n_row)])
        else:
            for d in range(CORES, n_row, CORES):
                got[d] = swap(value, d)
        for d in range(0, n_row, CORES):
            got[d + 1] = swap(got[d], 1)
        return [got[d] for d in range(n_row)]

    def body(three_centre, occupied, virtual, tile_map):
        columns = three_centre.shape[2]
        width = columns * n_col // n_row
        ab = columns // tile_map.shape[1]
        unit = width // sum(SHARES)
        keep = jnp.repeat(tile_map.astype(F32), ab, axis=1)
        row, z = lax.axis_index("row"), lax.axis_index("col")
        core, chip = row % CORES, row // CORES
        occupied, virtual = (pltpu.with_memory_space_constraint(a, pltpu.HBM) for a in (occupied, virtual))
        core_at = core.astype(jnp.int32)[None]
        place = jnp.stack([chip, z]).astype(jnp.int32)

        chunks, right_groups = [], []
        for tag, first, shares in (("_a", 0, SHARES[:2]), ("_b", sum(SHARES[:2]), SHARES[2:])):
            o, v = stage_one(core_at, three_centre, occupied, virtual, keep, unit, width, first, shares)
            chunks += o
            right_groups.append((tag, first, v))

        right = []
        for tag, first, v in right_groups:
            pieces = gather_rows(v, core)
            right.append((first * unit, *split_rows(pieces)))

        out, at = None, 0
        for j, (share, (theirs, ours)) in enumerate(zip(SHARES, chunks)):
            tag = "_" + str(j)
            other = swap(theirs, 1)
            both = jnp.stack([ours, other])
            sources = along_columns(both, j in DIRECT)
            blocks = choose(place, sources, chips)
            mine = [blocks[0]]
            for d in range(1, chips):
                mine.append(swap(blocks[d], CORES * d))
            out = product_rows(mine, right, out, width, width, unit, at * unit)
            at += share
        return out

    return jax.shard_map(
        body,
        mesh=mesh,
        in_specs=(
            P("row", None, "col"),
            P("row", None, None),
            P("row", None, None),
            P("row", "col"),
        ),
        out_specs=P("row", "col"),
        check_vma=False,
    )
```
